256 devices in a mesh: pair: 64 (over x, y_hi, z), tm: 4 (over y_lo, core).
Axes of the slice: x: 4, y: 4 (y_hi: 2, y_lo: 2; y = y_hi * 2 + y_lo), z: 8, core: 2. Of those that a mesh axis runs over, the one named last changes fastest.
Arguments:
- history: float32 [8192, 32768], P('tm', 'pair'), may hold values from -6 to 6
- round_index: int32 [1], replicated, may hold values from 0 to 126
Outputs:
- rotated: float32 [8192, 32768], P('tm', 'pair')
The draws below stay inside these ranges and needn't reach their ends.
Inputs may be any that keep to these rules, and one draw needn't show every extreme that they name: `round_index`: the same value on every device.
All inputs are finite; a program needn't handle non-finite values.
Results may differ from the reference program's by a relative error of at most 0.0003.
Values sent between devices are 32-bit elements; how exact they have to be, the bound alone decides.
A program may use at most 64 MiB of HBM per device.

```python
import jax
import jax.numpy as jnp
from jax import lax

COLS = 256
STEPS = 4
SAMPLES = 8192
TAGS = 32768
N_PAIR = 64


def levels(own_key, shape, cuts, smallest, high):
    gain = 1.0
    for axis_at, parts in cuts:
        draws = jax.random.uniform(jax.random.fold_in(jax.random.fold_in(own_key, 6), axis_at), (parts,), jnp.float32, smallest / len(cuts), high / len(cuts))
        gain = gain * jnp.repeat(jnp.exp(draws), shape[axis_at] // parts).reshape((-1,) + (1,) * (len(shape) - 1 - axis_at))
    return gain


def normal_values(rng, extent, scale, most, cuts=(), held_as=jnp.bfloat16):
    factor_of = levels(rng, extent, cuts, -0.22, 0.18) if cuts else 1.0
    entries = jax.random.normal(rng, extent, jnp.float32) * scale * factor_of
    return jnp.minimum(jnp.maximum(entries, -most), most).astype(held_as)


def setup_inputs(seed: int = 0) -> dict:
    key_of = jax.random.split(jax.random.key(seed), 3)
    return {
        "history": normal_values(key_of[0], (SAMPLES, TAGS), 1.0, 6.0, ((0, 4), (1, 64)), jnp.float32),
        "round_index": jax.random.randint(key_of[1], (1,), 0, 2 * N_PAIR - 1).astype(jnp.int32),
    }


epsilon = 1e-06

def block_ids(round_index, pair_count):
    position = jnp.arange(pair_count, dtype=jnp.int32)
    cycle_len = 2 * pair_count - 1
    round_now = round_index[0].astype(jnp.int32)
    top_ids = jnp.where(position == 0, 0, 1 + jnp.mod(position - 1 - round_now, cycle_len)).astype(jnp.int32)
    bottom_ids = (1 + jnp.mod(2 * pair_count - 2 - position - round_now, cycle_len)).astype(jnp.int32)
    return (top_ids, bottom_ids)

def orientation(top_id, bottom_id, width):
    column = jnp.arange(2 * width, dtype=jnp.int32)
    global_id = jnp.where(column < width, top_id * width + column, bottom_id * width + column - width)
    return jnp.sign(global_id[None, :] - global_id[:, None]).astype(jnp.float32)

def start_iterate(gram_full, orient):
    diag_sq = jnp.diagonal(gram_full)
    skew_part = orient * gram_full / (diag_sq[:, None] + diag_sq[None, :] + epsilon)
    scale_norm = jnp.sqrt(1.0 + jnp.sum(skew_part * skew_part))
    identity = jnp.eye(gram_full.shape[0], dtype=jnp.float32)
    return (identity + skew_part) / scale_norm

def polar_step(factor):
    identity = jnp.eye(factor.shape[1], dtype=jnp.float32)
    square = jnp.dot(factor.T, factor, precision=lax.Precision.HIGHEST, preferred_element_type=jnp.float32)
    return jnp.dot(factor, 1.5 * identity - 0.5 * square, precision=lax.Precision.HIGHEST, preferred_element_type=jnp.float32)

def reference(history, round_index):
    pair_count = N_PAIR
    width = COLS
    blocks = history.reshape(SAMPLES, pair_count, 2 * width).transpose(1, 0, 2)
    top_ids, bottom_ids = block_ids(round_index, pair_count)

    def rotate_pair(inputs):
        columns, top_id, bottom_id = inputs
        gram_full = jnp.dot(columns.T, columns, precision=lax.Precision.HIGHEST, preferred_element_type=jnp.float32)
        factor = start_iterate(gram_full, orientation(top_id, bottom_id, width))
        for step in range(STEPS):
            factor = polar_step(factor)
        return jnp.dot(columns, factor, precision=lax.Precision.HIGHEST, preferred_element_type=jnp.float32)
    rotated = lax.map(rotate_pair, (blocks, top_ids, bottom_ids))
    top_out = rotated[:, :, :width]
    bottom_out = rotated[:, :, width:]
    new_top = jnp.concatenate([top_out[:1], bottom_out[:1], top_out[1:-1]], axis=0)
    new_bottom = jnp.concatenate([bottom_out[1:], top_out[-1:]], axis=0)
    joined = jnp.concatenate([new_top, new_bottom], axis=2)
    return joined.transpose(1, 0, 2).reshape(SAMPLES, TAGS)
```

```python
import functools

import jax
import jax.numpy as jnp
from jax import lax
from jax.experimental import pallas as pl
from jax.experimental.pallas import tpu as pltpu
from jax.sharding import PartitionSpec as P

STEPS = 4
EPS = 1e-06
T = 128
BLOCKS = [(i, j) for i in range(4) for j in range(i, 4)]
OWN = [BLOCKS[:5], BLOCKS[5:]]
CHUNKS = 8
MESH = pl.DeviceIdType.MESH
F32 = jnp.float32
BF16 = jnp.bfloat16


def split(value):
    high = value.astype(BF16)
    return high, (value - high.astype(F32)).astype(BF16)


def dot(a, b):
    return jnp.dot(a, b, preferred_element_type=F32)


def dot_t(a, b):
    return lax.dot_general(a, b, (((0,), (0,)), ((), ())), preferred_element_type=F32)


def kernel(
    round_ref, hist, top, bot,
    stage, bh, bl, hh, mm, part, fin, recv_a, recv_b, x, xh, xl, ph, pm, out_r, out_l,
    load_sem, a_sem, b_sem, c_sem, r_send, l_send, r_recv, l_recv,
):
    rows, cols = hist.shape
    width = cols // 2
    step_rows = rows // CHUNKS
    pair_count = lax.axis_size("pair")
    pos = lax.axis_index("pair")
    tm = lax.axis_index("tm")
    core = lax.rem(tm, 2)
    sibling = {"tm": tm + 1 - 2 * core}
    across = {"tm": lax.rem(tm + 2, 4)}
    right = {"pair": jnp.minimum(pos + 1, pair_count - 1)}
    left = {"pair": jnp.maximum(pos - 1, 0)}
    has_right = pos < pair_count - 1
    has_left = pos > 0

    def load(i):
        rs = pl.ds(i * step_rows, step_rows)
        return pltpu.make_async_copy(hist.at[rs], stage.at[rs], load_sem.at[i])

    for i in range(CHUNKS):
        load(i).start()

    barrier = pltpu.get_barrier_semaphore()
    for target in (sibling, across):
        pl.semaphore_signal(barrier, inc=1, device_id=target, device_id_type=MESH)

    @pl.when(has_right)
    def _():
        pl.semaphore_signal(barrier, inc=1, device_id=right, device_id_type=MESH)

    @pl.when(has_left)
    def _():
        pl.semaphore_signal(barrier, inc=1, device_id=left, device_id_type=MESH)

    for i in range(CHUNKS):
        load(i).wait()
        rs = pl.ds(i * step_rows, step_rows)
        h, l = split(stage[rs, :])
        bh[rs, :] = h
        bl[rs, :] = l
        g_top = dot_t(h[:, :width], h)
        g_bot = dot_t(h[:, width:], h[:, width:])
        m_new = dot_t(h, l)
        if i == 0:
            hh[:width, :] = g_top
            hh[width:, width:] = g_bot
            mm[...] = m_new
        else:
            hh[:width, :] += g_top
            hh[width:, width:] += g_bot
            mm[...] += m_new

    for k, (i, j) in enumerate(BLOCKS):
        si, sj = pl.ds(i * T, T), pl.ds(j * T, T)
        part[k] = hh[si, sj] + (mm[si, sj] + mm[sj, si].T)

    peers = 2 + has_right.astype(jnp.int32) + has_left.astype(jnp.int32)
    pl.semaphore_wait(barrier, peers)

    half = len(BLOCKS) // 2
    mine, other = core * half, (1 - core) * half

    swap = pltpu.make_async_remote_copy(
        part.at[pl.ds(other, half)], recv_a, a_sem.at[0], a_sem.at[1],
        device_id=sibling, device_id_type=MESH,
    )
    swap.start()

    def cross(k):
        return pltpu.make_async_remote_copy(
            part.at[mine + k], recv_b.at[k], b_sem.at[0, k], b_sem.at[1, k],
            device_id=across, device_id_type=MESH,
        )

    def share(k, offset):
        return pltpu.make_async_remote_copy(
            fin.at[offset + k], fin.at[offset + k], c_sem.at[0, k], c_sem.at[1, k],
            device_id=sibling, device_id_type=MESH,
        )

    swap.wait()
    for k in range(half):
        part[mine + k] = part[mine + k] + recv_a[k]
        cross(k).start()
    for k in range(half):
        cross(k).wait_recv()
        fin[mine + k] = part[mine + k] + recv_b[k]
        share(k, mine).start()
    for k in range(half):
        share(k, other).wait_recv()

    cycle = 2 * pair_count - 1
    now = round_ref[0]

    def wrap(value):
        return lax.rem(lax.rem(value, cycle) + cycle, cycle)

    top_id = jnp.where(pos == 0, 0, 1 + wrap(pos - 1 - now))
    bottom_id = 1 + wrap(2 * pair_count - 2 - pos - now)
    sign = jnp.where(top_id < bottom_id, 1.0, -1.0).astype(F32)
    row_at = lax.broadcasted_iota(jnp.int32, (T, T), 0)
    col_at = lax.broadcasted_iota(jnp.int32, (T, T), 1)
    on_diag = row_at == col_at
    within = jnp.where(row_at < col_at, 1.0, jnp.where(on_diag, 0.0, -1.0)).astype(F32)
    along, down = [], []
    for i in range(4):
        d = jnp.where(on_diag, fin[BLOCKS.index((i, i))], 0.0)
        along.append(jnp.sum(d, axis=0, keepdims=True))
        down.append(jnp.sum(d, axis=1, keepdims=True))
    total = jnp.zeros((T, T), F32)
    for k, (i, j) in enumerate(BLOCKS):
        si, sj = pl.ds(i * T, T), pl.ds(j * T, T)
        value = fin[k] / (down[i] + along[j] + EPS)
        if i == j:
            value = value * within
            total = total + value * value
            x[si, sj] = value
        else:
            if i < 2 <= j:
                value = value * sign
            total = total + 2.0 * (value * value)
            x[si, sj] = value
            x[sj, si] = -value.T
    scale = 1.0 / jnp.sqrt(1.0 + jnp.sum(total, keepdims=True))
    wide_eye = (
        lax.broadcasted_iota(jnp.int32, (cols, cols), 0)
        == lax.broadcasted_iota(jnp.int32, (cols, cols), 1)
    )
    start = (x[...] + jnp.where(wide_eye, 1.0, 0.0)) * scale
    x[...] = start
    h, l = split(start)
    xh[...] = h
    xl[...] = l

    def polar(step, carry):
        h, l = xh[...], xl[...]
        square = dot_t(h, h) + (dot_t(h, l) + dot_t(l, h))
        p = jnp.where(wide_eye, 1.5, 0.0) - 0.5 * square
        p_h, p_l = split(p)
        ph[...] = p_h
        pm[...] = p_l
        new = dot(xh[...], ph[...]) + (dot(xh[...], pm[...]) + dot(xl[...], ph[...]))
        n_h, n_l = split(new)
        xh[...] = n_h
        xl[...] = n_l
        return carry

    lax.fori_loop(0, STEPS, polar, 0)

    @pl.when(pos == 0)
    def _():
        ph[:, :width] = xh[:, width:]
        ph[:, width:] = xh[:, :width]
        pm[:, :width] = xl[:, width:]
        pm[:, width:] = xl[:, :width]

    @pl.when(pos > 0)
    def _():
        ph[...] = xh[...]
        pm[...] = xl[...]

    def to_right(i):
        rs = pl.ds(i * step_rows, step_rows)
        return pltpu.make_async_remote_copy(
            out_r.at[rs], top.at[rs], r_send.at[i], r_recv.at[i],
            device_id=right, device_id_type=MESH,
        )

    def to_left(i):
        rs = pl.ds(i * step_rows, step_rows)
        return pltpu.make_async_remote_copy(
            out_l.at[rs], bot.at[rs], l_send.at[i], l_recv.at[i],
            device_id=left, device_id_type=MESH,
        )

    def rotate(i, carry):
        rs = pl.ds(pl.multiple_of(i * step_rows, step_rows), step_rows)
        h, l = bh[rs, :], bl[rs, :]
        r = dot(h, ph[...]) + (dot(h, pm[...]) + dot(l, ph[...]))
        out_r[rs, :] = r[:, :width]
        out_l[rs, :] = r[:, width:]

        @pl.when(has_right)
        def _():
            to_right(i).start()

        @pl.when(jnp.logical_not(has_right))
        def _():
            pltpu.make_async_copy(out_r.at[rs], bot.at[rs], l_recv.at[i]).start()

        @pl.when(has_left)
        def _():
            to_left(i).start()

        @pl.when(jnp.logical_not(has_left))
        def _():
            pltpu.make_async_copy(out_l.at[rs], top.at[rs], r_recv.at[i]).start()

        return carry

    lax.fori_loop(0, CHUNKS, rotate, 0)

    for k in range(half):
        cross(k).wait_send()
        share(k, mine).wait_send()

    def finish(i, carry):
        @pl.when(has_right)
        def _():
            to_right(i).wait_send()

        @pl.when(has_left)
        def _():
            to_left(i).wait_send()

        to_right(i).wait_recv()
        to_left(i).wait_recv()
        return carry

    lax.fori_loop(0, CHUNKS, finish, 0)


def shards(history, round_index):
    rows, cols = history.shape
    width = cols // 2
    half = len(BLOCKS) // 2
    vmem = pltpu.VMEM
    dma = pltpu.SemaphoreType.DMA
    top, bot = pl.pallas_call(
        kernel,
        out_shape=[jax.ShapeDtypeStruct((rows, width), F32)] * 2,
        in_specs=[
            pl.BlockSpec(memory_space=pltpu.SMEM),
            pl.BlockSpec(memory_space=pl.ANY),
        ],
        out_specs=[pl.BlockSpec(memory_space=pl.ANY)] * 2,
        scratch_shapes=[
            vmem((rows, cols), F32),
            vmem((rows, cols), BF16),
            vmem((rows, cols), BF16),
            vmem((cols, cols), F32),
            vmem((cols, cols), F32),
            vmem((2 * half, T, T), F32),
            vmem((2 * half, T, T), F32),
            vmem((half, T, T), F32),
            vmem((half, T, T), F32),
            vmem((cols, cols), F32),
            vmem((cols, cols), BF16),
            vmem((cols, cols), BF16),
            vmem((cols, cols), BF16),
            vmem((cols, cols), BF16),
            vmem((rows, width), F32),
            vmem((rows, width), F32),
            dma((CHUNKS,)),
            dma((2,)),
            dma((2, half)),
            dma((2, half)),
            dma((CHUNKS,)),
            dma((CHUNKS,)),
            dma((CHUNKS,)),
            dma((CHUNKS,)),
        ],
        compiler_params=pltpu.CompilerParams(
            collective_id=0, has_side_effects=True, vmem_limit_bytes=48 * 1024 * 1024
        ),
        name="pairing_round",
    )(round_index, history)
    return jnp.concatenate([top, bot], axis=1)


def solution(mesh):
    in_specs = (P("tm", "pair"), P())
    out_specs = P("tm", "pair")
    return jax.shard_map(shards, mesh=mesh, in_specs=in_specs, out_specs=out_specs, check_vma=False)
```

```python
import functools

import jax
import jax.numpy as jnp
from jax import lax
from jax.experimental import pallas as pl
from jax.experimental.pallas import tpu as pltpu
from jax.sharding import PartitionSpec as P

STEPS = 4
EPS = 1e-06
T = 128
BLOCKS = [(0, 0), (0, 1), (2, 2), (2, 3), (0, 2), (0, 3), (1, 2), (1, 3)]
GROUPS = [(0, 2), (2, 2), (4, 2), (6, 2)]
CHUNKS = 8
PIECES = 4
MESH = pl.DeviceIdType.MESH
F32 = jnp.float32
BF16 = jnp.bfloat16


def split(value):
    high = value.astype(BF16)
    return high, (value - high.astype(F32)).astype(BF16)


def dot(a, b):
    return jnp.dot(a, b, preferred_element_type=F32)


def dot_nt(a, b):
    return lax.dot_general(a, b, (((1,), (1,)), ((), ())), preferred_element_type=F32)


def kernel(
    round_ref, hist, top, bot,
    stage, bh, bl, bt, part, fin, recv_a, recv_b, dv, x, xh, xl, ph, pm, out_r, out_l,
    load_sem, a_sem, b_sem, c_sem, d_sem, r_send, l_send, r_recv, l_recv,
):
    rows, cols = hist.shape
    width = cols // 2
    step_rows = rows // CHUNKS
    pair_count = lax.axis_size("pair")
    pos = lax.axis_index("pair")
    tm = lax.axis_index("tm")
    core = lax.rem(tm, 2)
    sibling = {"tm": tm + 1 - 2 * core}
    across = {"tm": lax.rem(tm + 2, 4)}
    right = {"pair": jnp.minimum(pos + 1, pair_count - 1)}
    left = {"pair": jnp.maximum(pos - 1, 0)}
    has_right = pos < pair_count - 1
    has_left = pos > 0

    def load(i):
        rs = pl.ds(i * step_rows, step_rows)
        return pltpu.make_async_copy(hist.at[rs], stage.at[rs], load_sem.at[i])

    for i in range(CHUNKS):
        load(i).start()

    barrier = pltpu.get_barrier_semaphore()
    for target in (sibling, across):
        pl.semaphore_signal(barrier, inc=1, device_id=target, device_id_type=MESH)

    @pl.when(has_right)
    def _():
        pl.semaphore_signal(barrier, inc=1, device_id=right, device_id_type=MESH)

    @pl.when(has_left)
    def _():
        pl.semaphore_signal(barrier, inc=1, device_id=left, device_id_type=MESH)

    lo, hi = pl.ds(0, width), pl.ds(width, width)
    first_high, first_low = None, None
    for i in range(CHUNKS):
        load(i).wait()
        rs = pl.ds(i * step_rows, step_rows)
        h, l = split(stage[rs, :])
        bh[rs, :] = h
        bl[rs, :] = l
        bt[:, rs] = h.T
        new_high = dot(bt[lo, rs], bh[rs, lo])
        new_low = dot(bt[lo, rs], bl[rs, lo])
        first_high = new_high if i == 0 else first_high + new_high
        first_low = new_low if i == 0 else first_low + new_low

    mine, other = pl.ds(core * (T // 2), T // 2), pl.ds((1 - core) * (T // 2), T // 2)

    def swap(g):
        group = pl.ds(*GROUPS[g])
        return pltpu.make_async_remote_copy(
            part.at[group, other], recv_a.at[group], a_sem.at[0, g], a_sem.at[1, g],
            device_id=sibling, device_id_type=MESH,
        )

    def cross(g):
        group = pl.ds(*GROUPS[g])
        return pltpu.make_async_remote_copy(
            part.at[group, mine], recv_b.at[group], b_sem.at[0, g], b_sem.at[1, g],
            device_id=across, device_id_type=MESH,
        )

    def share(g, rows_of):
        group = pl.ds(*GROUPS[g])
        return pltpu.make_async_remote_copy(
            fin.at[group, rows_of], fin.at[group, rows_of], c_sem.at[0, g], c_sem.at[1, g],
            device_id=sibling, device_id_type=MESH,
        )

    def send_on(g):
        swap(g).wait_recv()
        group = pl.ds(*GROUPS[g])
        part[group, mine] = part[group, mine] + recv_a[group]
        cross(g).start()

    row_at = lax.broadcasted_iota(jnp.int32, (T, T), 0)
    col_at = lax.broadcasted_iota(jnp.int32, (T, T), 1)
    on_diag = row_at == col_at
    upper, lower = row_at < col_at, row_at > col_at

    def diagonal(g, high, low):
        value = high + (low + low.T)
        second = value[T:, T:]
        part[2 * g] = jnp.where(lower, second, value[:T, :T])
        part[2 * g + 1] = value[:T, T:]
        dv[0, pl.ds(g, 1), :] = jnp.sum(jnp.where(on_diag, second, 0.0), axis=0, keepdims=True)

    def swap_d():
        return pltpu.make_async_remote_copy(
            dv.at[0], dv.at[1], d_sem.at[0], d_sem.at[1], device_id=sibling, device_id_type=MESH
        )

    def cross_d():
        return pltpu.make_async_remote_copy(
            dv.at[2], dv.at[3], d_sem.at[2], d_sem.at[3], device_id=across, device_id_type=MESH
        )

    dv[0] = jnp.zeros_like(dv[0])
    diagonal(0, first_high, first_low)
    peers = 2 + has_right.astype(jnp.int32) + has_left.astype(jnp.int32)
    pl.semaphore_wait(barrier, peers)
    swap(0).start()
    diagonal(1, dot(bt[hi, :], bh[:, hi]), dot(bt[hi, :], bl[:, hi]))
    swap(1).start()
    swap_d().start()
    send_on(0)
    off = dot(bt[lo, :], bh[:, hi]) + (dot(bt[lo, :], bl[:, hi]) + dot(bt[hi, :], bl[:, lo]).T)
    for k in range(4, 8):
        i, j = BLOCKS[k]
        part[k] = off[i * T : i * T + T, (j - 2) * T : (j - 1) * T]
    swap(2).start()
    swap(3).start()
    swap_d().wait_recv()
    dv[2] = dv[0] + dv[1]
    cross_d().start()
    for g in (1, 2, 3):
        send_on(g)

    def summed(g):
        cross(g).wait_recv()
        group = pl.ds(*GROUPS[g])
        fin[group, mine] = part[group, mine] + recv_b[group]
        share(g, mine).start()

    cycle = 2 * pair_count - 1
    now = round_ref[0]

    def wrap(value):
        return lax.rem(lax.rem(value, cycle) + cycle, cycle)

    top_id = jnp.where(pos == 0, 0, 1 + wrap(pos - 1 - now))
    bottom_id = 1 + wrap(2 * pair_count - 2 - pos - now)
    sign = jnp.where(top_id < bottom_id, 1.0, -1.0).astype(F32)
    along, down = [None] * 4, [None] * 4

    def diag_from(i, row):
        spread = jnp.where(on_diag, row, 0.0)
        along[i] = jnp.sum(spread, axis=0, keepdims=True)
        down[i] = jnp.sum(spread, axis=1, keepdims=True)

    total = jnp.zeros((T, T), F32)
    summed(0)
    cross_d().wait_recv()
    d_last = dv[2] + dv[3]
    for g in range(len(GROUPS)):
        if g + 1 < len(GROUPS):
            summed(g + 1)
        share(g, other).wait_recv()
        first, count = GROUPS[g]
        for k in range(first, first + count):
            i, j = BLOCKS[k]
            value = fin[k]
            if i == j:
                diag_from(i, value)
                diag_from(i + 1, d_last[g : g + 1, :])
                for m, keep in ((i, upper), (i + 1, lower)):
                    s = value / (down[m] + along[m] + EPS)
                    s = jnp.where(keep, s, 0.0)
                    if m > i:
                        s = -s
                    total = total + 2.0 * (s * s)
                    at = pl.ds(m * T, T)
                    x[at, at] = s - s.T
            else:
                si, sj = pl.ds(i * T, T), pl.ds(j * T, T)
                s = value / (down[i] + along[j] + EPS)
                if i < 2 <= j:
                    s = s * sign
                total = total + 2.0 * (s * s)
                x[si, sj] = s
                x[sj, si] = -s.T
    scale = 1.0 / jnp.sqrt(1.0 + jnp.sum(total, keepdims=True))
    wide_eye = (
        lax.broadcasted_iota(jnp.int32, (cols, cols), 0)
        == lax.broadcasted_iota(jnp.int32, (cols, cols), 1)
    )
    start = (x[...] + jnp.where(wide_eye, 1.0, 0.0)) * scale
    x[...] = start
    h, l = split(start)
    xh[...] = h
    xl[...] = l

    def put(r, c, value):
        h, l = split(value)
        ph[r, c] = h
        pm[r, c] = l

    narrow_eye = jnp.where(
        lax.broadcasted_iota(jnp.int32, (width, width), 0)
        == lax.broadcasted_iota(jnp.int32, (width, width), 1),
        1.5,
        0.0,
    )
    for step in range(STEPS):
        cross_part = dot_nt(xh[lo, :], xh[hi, :]) + (
            dot_nt(xh[lo, :], xl[hi, :]) + dot_nt(xl[lo, :], xh[hi, :])
        )
        cross_part = -0.5 * cross_part
        put(lo, hi, cross_part)
        put(hi, lo, cross_part.T)
        for r in (lo, hi):
            m = dot_nt(xh[r, :], xl[r, :])
            put(r, r, narrow_eye - 0.5 * (dot_nt(xh[r, :], xh[r, :]) + (m + m.T)))
        new = dot(xh[...], ph[...]) + (dot(xh[...], pm[...]) + dot(xl[...], ph[...]))
        h, l = split(new)
        xh[...] = h
        xl[...] = l

    @pl.when(pos == 0)
    def _():
        ph[:, :width] = xh[:, width:]
        ph[:, width:] = xh[:, :width]
        pm[:, :width] = xl[:, width:]
        pm[:, width:] = xl[:, :width]

    @pl.when(pos > 0)
    def _():
        ph[...] = xh[...]
        pm[...] = xl[...]

    def to_right(i):
        rs = pl.ds(i * step_rows, step_rows)
        return pltpu.make_async_remote_copy(
            out_r.at[rs], top.at[rs], r_send.at[i], r_recv.at[i],
            device_id=right, device_id_type=MESH,
        )

    def to_left(i):
        rs = pl.ds(i * step_rows, step_rows)
        return pltpu.make_async_remote_copy(
            out_l.at[rs], bot.at[rs], l_send.at[i], l_recv.at[i],
            device_id=left, device_id_type=MESH,
        )

    def rotate(i, carry):
        rs = pl.ds(pl.multiple_of(i * step_rows, step_rows), step_rows)
        h, l = bh[rs, :], bl[rs, :]
        r = dot(h, ph[...]) + (dot(h, pm[...]) + dot(l, ph[...]))
        out_r[rs, :] = r[:, :width]
        out_l[rs, :] = r[:, width:]

        @pl.when(has_right)
        def _():
            to_right(i).start()

        @pl.when(jnp.logical_not(has_right))
        def _():
            pltpu.make_async_copy(out_r.at[rs], bot.at[rs], l_recv.at[i]).start()

        @pl.when(has_left)
        def _():
            to_left(i).start()

        @pl.when(jnp.logical_not(has_left))
        def _():
            pltpu.make_async_copy(out_l.at[rs], top.at[rs], r_recv.at[i]).start()

        return carry

    lax.fori_loop(0, CHUNKS, rotate, 0)

    for g in range(len(GROUPS)):
        swap(g).wait_send()
        cross(g).wait_send()
        share(g, mine).wait_send()
    swap_d().wait_send()
    cross_d().wait_send()

    def finish(i, carry):
        @pl.when(has_right)
        def _():
            to_right(i).wait_send()

        @pl.when(has_left)
        def _():
            to_left(i).wait_send()

        to_right(i).wait_recv()
        to_left(i).wait_recv()
        return carry

    lax.fori_loop(0, CHUNKS, finish, 0)


def join(top, bot, out, sem):
    rows, width = top.shape
    copies = []
    for k in range(PIECES):
        rs = pl.ds(k * rows // PIECES, rows // PIECES)
        for i, half in enumerate((top, bot)):
            copies.append(
                pltpu.make_async_copy(
                    half.at[rs], out.at[rs, pl.ds(i * width, width)], sem.at[i, k]
                )
            )
    for copy in copies:
        copy.start()
    for copy in copies:
        copy.wait()


def shards(history, round_index):
    rows, cols = history.shape
    width = cols // 2
    vmem = pltpu.VMEM
    dma = pltpu.SemaphoreType.DMA
    top, bot = pl.pallas_call(
        kernel,
        out_shape=[jax.ShapeDtypeStruct((rows, width), F32)] * 2,
        in_specs=[
            pl.BlockSpec(memory_space=pltpu.SMEM),
            pl.BlockSpec(memory_space=pl.ANY),
        ],
        out_specs=[pl.BlockSpec(memory_space=pl.ANY)] * 2,
        scratch_shapes=[
            vmem((rows, cols), F32),
            vmem((rows, cols), BF16),
            vmem((rows, cols), BF16),
            vmem((cols, rows), BF16),
            vmem((len(BLOCKS), T, T), F32),
            vmem((len(BLOCKS), T, T), F32),
            vmem((len(BLOCKS), T // 2, T), F32),
            vmem((len(BLOCKS), T // 2, T), F32),
            vmem((4, 8, T), F32),
            vmem((cols, cols), F32),
            vmem((cols, cols), BF16),
            vmem((cols, cols), BF16),
            vmem((cols, cols), BF16),
            vmem((cols, cols), BF16),
            vmem((rows, width), F32),
            vmem((rows, width), F32),
            dma((CHUNKS,)),
            dma((2, len(GROUPS))),
            dma((2, len(GROUPS))),
            dma((2, len(GROUPS))),
            dma((4,)),
            dma((CHUNKS,)),
            dma((CHUNKS,)),
            dma((CHUNKS,)),
            dma((CHUNKS,)),
        ],
        compiler_params=pltpu.CompilerParams(
            collective_id=0, has_side_effects=True, vmem_limit_bytes=48 * 1024 * 1024
        ),
        name="pairing_round",
    )(round_index, history)
    return pl.pallas_call(
        join,
        out_shape=jax.ShapeDtypeStruct((rows, cols), F32),
        in_specs=[pl.BlockSpec(memory_space=pltpu.VMEM)] * 2,
        out_specs=pl.BlockSpec(memory_space=pl.ANY),
        scratch_shapes=[dma((2, PIECES))],
        compiler_params=pltpu.CompilerParams(vmem_limit_bytes=8 * 1024 * 1024),
        name="join",
    )(top, bot)


def solution(mesh):
    in_specs = (P("tm", "pair"), P())
    out_specs = P("tm", "pair")
    return jax.shard_map(shards, mesh=mesh, in_specs=in_specs, out_specs=out_specs, check_vma=False)
```

```python
import functools

import jax
import jax.numpy as jnp
from jax import lax
from jax.experimental import pallas as pl
from jax.experimental.pallas import tpu as pltpu
from jax.sharding import PartitionSpec as P

STEPS = 4
EPS = 1e-06
T = 128
BLOCKS = [(0, 0), (0, 1), (2, 2), (2, 3), (0, 2), (0, 3), (1, 2), (1, 3)]
GROUPS = [(0, 2), (2, 2), (4, 2), (6, 2)]
DIRECT = 1
CHUNKS = 8
LOADS = 4
PIECES = 4
MESH = pl.DeviceIdType.MESH
F32 = jnp.float32
BF16 = jnp.bfloat16


def split(value):
    high = value.astype(BF16)
    return high, (value - high.astype(F32)).astype(BF16)


def dot(a, b):
    return jnp.dot(a, b, preferred_element_type=F32)


def dot_nt(a, b):
    return lax.dot_general(a, b, (((1,), (1,)), ((), ())), preferred_element_type=F32)


def kernel(
    round_ref, hist, top, bot,
    stage, bh, bl, bt, part, fin, recv_a, recv_b, recv_0, dv, xh, xl, ph, pm, out_r, out_l,
    load_sem, a_sem, b_sem, o_sem, c_sem, d_sem, r_send, l_send, r_recv, l_recv,
):
    rows, cols = hist.shape
    width = cols // 2
    step_rows = rows // CHUNKS
    load_rows = rows // LOADS
    pair_count = lax.axis_size("pair")
    pos = lax.axis_index("pair")
    tm = lax.axis_index("tm")
    core = lax.rem(tm, 2)
    sibling = {"tm": tm + 1 - 2 * core}
    across = {"tm": lax.rem(tm + 2, 4)}
    opposite = {"tm": 3 - tm}
    right = {"pair": jnp.minimum(pos + 1, pair_count - 1)}
    left = {"pair": jnp.maximum(pos - 1, 0)}
    has_right = pos < pair_count - 1
    has_left = pos > 0

    def load(i):
        rs = pl.ds(i * load_rows, load_rows)
        return pltpu.make_async_copy(hist.at[rs], stage.at[rs], load_sem.at[i])

    for i in range(LOADS):
        load(i).start()

    barrier = pltpu.get_barrier_semaphore()
    for target in (sibling, across, opposite):
        pl.semaphore_signal(barrier, inc=1, device_id=target, device_id_type=MESH)

    @pl.when(has_right)
    def _():
        pl.semaphore_signal(barrier, inc=1, device_id=right, device_id_type=MESH)

    @pl.when(has_left)
    def _():
        pl.semaphore_signal(barrier, inc=1, device_id=left, device_id_type=MESH)

    lo, hi = pl.ds(0, width), pl.ds(width, width)
    first_high, first_low = None, None
    for i in range(LOADS):
        load(i).wait()
        rs = pl.ds(i * load_rows, load_rows)
        h, l = split(stage[rs, :])
        bh[rs, :] = h
        bl[rs, :] = l
        bt[:, rs] = h.T
        new_high = dot(bt[lo, rs], bh[rs, lo])
        new_low = dot(bt[lo, rs], bl[rs, lo])
        first_high = new_high if i == 0 else first_high + new_high
        first_low = new_low if i == 0 else first_low + new_low

    mine, other = core, 1 - core

    def swap(g):
        group = pl.ds(*GROUPS[g])
        return pltpu.make_async_remote_copy(
            part.at[other, group], recv_a.at[group], a_sem.at[0, g], a_sem.at[1, g],
            device_id=sibling, device_id_type=MESH,
        )

    def straight(k):
        return pltpu.make_async_remote_copy(
            part.at[(mine, other)[k], 0], recv_0.at[k], o_sem.at[0, k], o_sem.at[1, k],
            device_id=(across, opposite)[k], device_id_type=MESH,
        )

    def crossing(g):
        first, count = GROUPS[g]
        return pl.ds(max(first, DIRECT), first + count - max(first, DIRECT))

    def cross(g):
        group = crossing(g)
        return pltpu.make_async_remote_copy(
            part.at[mine, group], recv_b.at[group], b_sem.at[0, g], b_sem.at[1, g],
            device_id=across, device_id_type=MESH,
        )

    def share(g, half):
        group = pl.ds(*GROUPS[g])
        return pltpu.make_async_remote_copy(
            fin.at[half, group], fin.at[half, group], c_sem.at[0, g], c_sem.at[1, g],
            device_id=sibling, device_id_type=MESH,
        )

    def send_on(g):
        swap(g).wait_recv()
        group = crossing(g)
        part[mine, group] = part[mine, group] + recv_a[group]
        cross(g).start()

    row_at = lax.broadcasted_iota(jnp.int32, (T, T), 0)
    col_at = lax.broadcasted_iota(jnp.int32, (T, T), 1)
    on_diag = row_at == col_at
    upper, lower = row_at < col_at, row_at > col_at

    def keep(k, value):
        part[0, k] = value[: T // 2]
        part[1, k] = value[T // 2 :]

    def diagonal(g, high, low):
        value = high + (low + low.T)
        second = value[T:, T:]
        keep(2 * g, jnp.where(lower, second, value[:T, :T]))
        keep(2 * g + 1, value[:T, T:])
        dv[0, pl.ds(g, 1), :] = jnp.sum(jnp.where(on_diag, second, 0.0), axis=0, keepdims=True)

    def send_d(k):
        return pltpu.make_async_remote_copy(
            dv.at[0], dv.at[1 + k], d_sem.at[0, k], d_sem.at[1, k],
            device_id=(sibling, across, opposite)[k], device_id_type=MESH,
        )

    dv[0] = jnp.zeros_like(dv[0])
    diagonal(0, first_high, first_low)
    peers = 3 + has_right.astype(jnp.int32) + has_left.astype(jnp.int32)
    pl.semaphore_wait(barrier, peers)
    for k in range(2):
        straight(k).start()
    swap(0).start()
    diagonal(1, dot(bt[hi, :], bh[:, hi]), dot(bt[hi, :], bl[:, hi]))
    swap(1).start()
    for k in range(3):
        send_d(k).start()
    send_on(0)
    off = dot(bt[lo, :], bh[:, hi]) + (dot(bt[lo, :], bl[:, hi]) + dot(bt[hi, :], bl[:, lo]).T)
    for k in range(4, 8):
        i, j = BLOCKS[k]
        keep(k, off[i * T : i * T + T, (j - 2) * T : (j - 1) * T])
    swap(2).start()
    swap(3).start()
    for g in (1, 2, 3):
        send_on(g)

    def summed(g):
        if g == 0:
            for k in range(2):
                straight(k).wait_recv()
            fin[mine, 0] = (part[mine, 0] + recv_a[0]) + (recv_0[0] + recv_0[1])
        cross(g).wait_recv()
        group = crossing(g)
        fin[mine, group] = part[mine, group] + recv_b[group]
        share(g, mine).start()

    cycle = 2 * pair_count - 1
    now = round_ref[0]

    def wrap(value):
        return lax.rem(lax.rem(value, cycle) + cycle, cycle)

    top_id = jnp.where(pos == 0, 0, 1 + wrap(pos - 1 - now))
    bottom_id = 1 + wrap(2 * pair_count - 2 - pos - now)
    sign = jnp.where(top_id < bottom_id, 1.0, -1.0).astype(F32)
    along, down = [None] * 4, [None] * 4

    def diag_from(i, row):
        spread = jnp.where(on_diag, row, 0.0)
        along[i] = jnp.sum(spread, axis=0, keepdims=True)
        down[i] = jnp.sum(spread, axis=1, keepdims=True)

    def place(r, c, value):
        h, l = split(value)
        xh[r, c] = h
        xl[r, c] = l

    total = jnp.zeros((T, T), F32)
    summed(0)
    for k in range(3):
        send_d(k).wait_recv()
    d_last = (dv[0] + dv[1]) + (dv[2] + dv[3])
    for g in range(len(GROUPS)):
        if g + 1 < len(GROUPS):
            summed(g + 1)
        share(g, other).wait_recv()
        first, count = GROUPS[g]
        for k in range(first, first + count):
            i, j = BLOCKS[k]
            value = jnp.concatenate([fin[0, k], fin[1, k]], axis=0)
            if i == j:
                diag_from(i, value)
                diag_from(i + 1, d_last[g : g + 1, :])
                for m, side in ((i, upper), (i + 1, lower)):
                    s = value / (down[m] + along[m] + EPS)
                    s = jnp.where(side, s, 0.0)
                    if m > i:
                        s = -s
                    total = total + 2.0 * (s * s)
                    at = pl.ds(m * T, T)
                    place(at, at, s - s.T)
            else:
                si, sj = pl.ds(i * T, T), pl.ds(j * T, T)
                s = value / (down[i] + along[j] + EPS)
                if i < 2 <= j:
                    s = s * sign
                total = total + 2.0 * (s * s)
                place(si, sj, s)
                place(sj, si, -s.T)
    norm = 1.0 + jnp.sum(total, keepdims=True)
    scale = 1.0 / jnp.sqrt(norm)
    scale_sq = 1.0 / norm

    def put(r, c, value):
        h, l = split(value)
        ph[r, c] = h
        pm[r, c] = l

    def eye(size):
        return lax.broadcasted_iota(jnp.int32, (size, size), 0) == lax.broadcasted_iota(
            jnp.int32, (size, size), 1
        )

    narrow_eye = eye(width)
    for step in range(STEPS):
        weight = -0.5 * scale_sq if step == 0 else -0.5
        on = 1.5 - 0.5 * scale_sq if step == 0 else 1.5
        cross_part = dot_nt(xh[lo, :], xh[hi, :]) + (
            dot_nt(xh[lo, :], xl[hi, :]) + dot_nt(xl[lo, :], xh[hi, :])
        )
        cross_part = weight * cross_part
        put(lo, hi, cross_part)
        put(hi, lo, cross_part.T)
        for r in (lo, hi):
            m = dot_nt(xh[r, :], xl[r, :])
            square = dot_nt(xh[r, :], xh[r, :]) + (m + m.T)
            put(r, r, jnp.where(narrow_eye, on, 0.0) + weight * square)
        new = None
        for c in (lo, hi):
            more = dot(xh[:, c], ph[c, :]) + (dot(xl[:, c], ph[c, :]) + dot(xh[:, c], pm[c, :]))
            new = more if new is None else new + more
        if step == 0:
            new = scale * (new + (ph[...].astype(F32) + pm[...].astype(F32)))
        h, l = split(new)
        xh[...] = h
        xl[...] = l

    def to_right(i, source=out_r):
        rs = pl.ds(i * step_rows, step_rows)
        return pltpu.make_async_remote_copy(
            source.at[rs], top.at[rs], r_send.at[i], r_recv.at[i],
            device_id=right, device_id_type=MESH,
        )

    def to_left(i):
        rs = pl.ds(i * step_rows, step_rows)
        return pltpu.make_async_remote_copy(
            out_l.at[rs], bot.at[rs], l_send.at[i], l_recv.at[i],
            device_id=left, device_id_type=MESH,
        )

    def rotated(i, columns):
        rs = pl.ds(pl.multiple_of(i * step_rows, step_rows), step_rows)
        h, l = bh[rs, :], bl[rs, :]
        w_h, w_l = xh[:, columns], xl[:, columns]
        return rs, dot(h, w_h) + (dot(h, w_l) + dot(l, w_h))

    def rotate_top(i, carry):
        rs, r = rotated(i, lo)
        out_r[rs, :] = r

        @pl.when(jnp.logical_and(has_left, has_right))
        def _():
            to_right(i).start()

        @pl.when(jnp.logical_not(has_right))
        def _():
            pltpu.make_async_copy(out_r.at[rs], bot.at[rs], l_recv.at[i]).start()

        @pl.when(jnp.logical_not(has_left))
        def _():
            pltpu.make_async_copy(out_r.at[rs], top.at[rs], r_recv.at[i]).start()

        return carry

    lax.fori_loop(0, CHUNKS, rotate_top, 0)

    def rotate_bottom(i, carry):
        rs, r = rotated(i, hi)
        out_l[rs, :] = r

        @pl.when(has_left)
        def _():
            to_left(i).start()

        @pl.when(jnp.logical_not(has_left))
        def _():
            to_right(i, out_l).start()

        return carry

    lax.fori_loop(0, CHUNKS, rotate_bottom, 0)

    for g in range(len(GROUPS)):
        swap(g).wait_send()
        cross(g).wait_send()
        share(g, mine).wait_send()
    for k in range(2):
        straight(k).wait_send()
    for k in range(3):
        send_d(k).wait_send()

    def finish(i, carry):
        @pl.when(has_right)
        def _():
            to_right(i).wait_send()

        @pl.when(has_left)
        def _():
            to_left(i).wait_send()

        to_right(i).wait_recv()
        to_left(i).wait_recv()
        return carry

    lax.fori_loop(0, CHUNKS, finish, 0)


def join(top, bot, out, sem):
    rows, width = top.shape
    copies = []
    for k in range(PIECES):
        rs = pl.ds(k * rows // PIECES, rows // PIECES)
        for i, half in enumerate((top, bot)):
            copies.append(
                pltpu.make_async_copy(
                    half.at[rs], out.at[rs, pl.ds(i * width, width)], sem.at[i, k]
                )
            )
    for copy in copies:
        copy.start()
    for copy in copies:
        copy.wait()


def shards(history, round_index):
    rows, cols = history.shape
    width = cols // 2
    vmem = pltpu.VMEM
    dma = pltpu.SemaphoreType.DMA
    top, bot = pl.pallas_call(
        kernel,
        out_shape=[jax.ShapeDtypeStruct((rows, width), F32)] * 2,
        in_specs=[
            pl.BlockSpec(memory_space=pltpu.SMEM),
            pl.BlockSpec(memory_space=pl.ANY),
        ],
        out_specs=[pl.BlockSpec(memory_space=pl.ANY)] * 2,
        scratch_shapes=[
            vmem((rows, cols), F32),
            vmem((rows, cols), BF16),
            vmem((rows, cols), BF16),
            vmem((cols, rows), BF16),
            vmem((2, len(BLOCKS), T // 2, T), F32),
            vmem((2, len(BLOCKS), T // 2, T), F32),
            vmem((len(BLOCKS), T // 2, T), F32),
            vmem((len(BLOCKS), T // 2, T), F32),
            vmem((2, T // 2, T), F32),
            vmem((4, 8, T), F32),
            vmem((cols, cols), BF16),
            vmem((cols, cols), BF16),
            vmem((cols, cols), BF16),
            vmem((cols, cols), BF16),
            vmem((rows, width), F32),
            vmem((rows, width), F32),
            dma((LOADS,)),
            dma((2, len(GROUPS))),
            dma((2, len(GROUPS))),
            dma((2, 2)),
            dma((2, len(GROUPS))),
            dma((2, 3)),
            dma((CHUNKS,)),
            dma((CHUNKS,)),
            dma((CHUNKS,)),
            dma((CHUNKS,)),
        ],
        compiler_params=pltpu.CompilerParams(
            collective_id=0, has_side_effects=True, vmem_limit_bytes=48 * 1024 * 1024
        ),
        name="pairing_round",
    )(round_index, history)
    return pl.pallas_call(
        join,
        out_shape=jax.ShapeDtypeStruct((rows, cols), F32),
        in_specs=[pl.BlockSpec(memory_space=pltpu.VMEM)] * 2,
        out_specs=pl.BlockSpec(memory_space=pl.ANY),
        scratch_shapes=[dma((2, PIECES))],
        compiler_params=pltpu.CompilerParams(vmem_limit_bytes=8 * 1024 * 1024),
        name="join",
    )(top, bot)


def solution(mesh):
    in_specs = (P("tm", "pair"), P())
    out_specs = P("tm", "pair")
    return jax.shard_map(shards, mesh=mesh, in_specs=in_specs, out_specs=out_specs, check_vma=False)
```

```python
import functools

import jax
import jax.numpy as jnp
from jax import lax
from jax.experimental import pallas as pl
from jax.experimental.pallas import tpu as pltpu
from jax.sharding import PartitionSpec as P

STEPS = 4
EPS = 1e-06
T = 128
BLOCKS = [(0, 0), (0, 1), (2, 2), (2, 3), (0, 2), (0, 3), (1, 2), (1, 3)]
GROUPS = [(0, 2), (2, 2), (4, 3), (7, 1)]
DIRECT = 1
CHUNKS = 8
LOADS = 4
PIECES = 4
MESH = pl.DeviceIdType.MESH
F32 = jnp.float32
BF16 = jnp.bfloat16


def split(value):
    high = value.astype(BF16)
    return high, (value - high.astype(F32)).astype(BF16)


def dot(a, b):
    return jnp.dot(a, b, preferred_element_type=F32)


def dot_nt(a, b):
    return lax.dot_general(a, b, (((1,), (1,)), ((), ())), preferred_element_type=F32)


def kernel(
    round_ref, hist, top, bot,
    stage, bh, bl, bt, part, fin, recv_a, recv_b, recv_0, dv, xh, xl, ph, pm, out_r, out_l,
    load_sem, a_sem, b_sem, o_sem, c_sem, d_sem, r_send, l_send, r_recv, l_recv,
):
    rows, cols = hist.shape
    width = cols // 2
    step_rows = rows // CHUNKS
    load_rows = rows // LOADS
    pair_count = lax.axis_size("pair")
    pos = lax.axis_index("pair")
    tm = lax.axis_index("tm")
    core = lax.rem(tm, 2)
    sibling = {"tm": tm + 1 - 2 * core}
    across = {"tm": lax.rem(tm + 2, 4)}
    opposite = {"tm": 3 - tm}
    right = {"pair": jnp.minimum(pos + 1, pair_count - 1)}
    left = {"pair": jnp.maximum(pos - 1, 0)}
    has_right = pos < pair_count - 1
    has_left = pos > 0

    def load(i):
        rs = pl.ds(i * load_rows, load_rows)
        return pltpu.make_async_copy(hist.at[rs], stage.at[rs], load_sem.at[i])

    for i in range(LOADS):
        load(i).start()

    barrier = pltpu.get_barrier_semaphore()
    for target in (sibling, across, opposite):
        pl.semaphore_signal(barrier, inc=1, device_id=target, device_id_type=MESH)

    @pl.when(has_right)
    def _():
        pl.semaphore_signal(barrier, inc=1, device_id=right, device_id_type=MESH)

    @pl.when(has_left)
    def _():
        pl.semaphore_signal(barrier, inc=1, device_id=left, device_id_type=MESH)

    lo, hi = pl.ds(0, width), pl.ds(width, width)
    first_high, first_low = None, None
    for i in range(LOADS):
        load(i).wait()
        rs = pl.ds(i * load_rows, load_rows)
        h, l = split(stage[rs, :])
        bh[rs, :] = h
        bl[rs, :] = l
        bt[:, rs] = h.T
        new_high = dot(bt[lo, rs], bh[rs, lo])
        new_low = dot(bt[lo, rs], bl[rs, lo])
        first_high = new_high if i == 0 else first_high + new_high
        first_low = new_low if i == 0 else first_low + new_low

    mine, other = core, 1 - core

    def swap(g):
        group = pl.ds(*GROUPS[g])
        return pltpu.make_async_remote_copy(
            part.at[other, group], recv_a.at[group], a_sem.at[0, g], a_sem.at[1, g],
            device_id=sibling, device_id_type=MESH,
        )

    def straight(k):
        return pltpu.make_async_remote_copy(
            part.at[(mine, other)[k], 0], recv_0.at[k], o_sem.at[0, k], o_sem.at[1, k],
            device_id=(across, opposite)[k], device_id_type=MESH,
        )

    def crossing(g):
        first, count = GROUPS[g]
        return pl.ds(max(first, DIRECT), first + count - max(first, DIRECT))

    def cross(g):
        group = crossing(g)
        return pltpu.make_async_remote_copy(
            part.at[mine, group], recv_b.at[group], b_sem.at[0, g], b_sem.at[1, g],
            device_id=across, device_id_type=MESH,
        )

    def share(g, half):
        group = pl.ds(*GROUPS[g])
        return pltpu.make_async_remote_copy(
            fin.at[half, group], fin.at[half, group], c_sem.at[0, g], c_sem.at[1, g],
            device_id=sibling, device_id_type=MESH,
        )

    def send_on(g):
        swap(g).wait_recv()
        group = crossing(g)
        part[mine, group] = part[mine, group] + recv_a[group]
        cross(g).start()

    row_at = lax.broadcasted_iota(jnp.int32, (T, T), 0)
    col_at = lax.broadcasted_iota(jnp.int32, (T, T), 1)
    on_diag = row_at == col_at
    upper, lower = row_at < col_at, row_at > col_at

    def keep(k, value):
        part[0, k] = value[: T // 2]
        part[1, k] = value[T // 2 :]

    def diagonal(g, high, low):
        value = high + (low + low.T)
        second = value[T:, T:]
        keep(2 * g, jnp.where(lower, second, value[:T, :T]))
        keep(2 * g + 1, value[:T, T:])
        dv[0, pl.ds(g, 1), :] = jnp.sum(jnp.where(on_diag, second, 0.0), axis=0, keepdims=True)

    def send_d(k):
        return pltpu.make_async_remote_copy(
            dv.at[0], dv.at[1 + k], d_sem.at[0, k], d_sem.at[1, k],
            device_id=(sibling, across, opposite)[k], device_id_type=MESH,
        )

    dv[0] = jnp.zeros_like(dv[0])
    diagonal(0, first_high, first_low)
    peers = 3 + has_right.astype(jnp.int32) + has_left.astype(jnp.int32)
    pl.semaphore_wait(barrier, peers)
    for k in range(2):
        straight(k).start()
    swap(0).start()
    diagonal(1, dot(bt[hi, :], bh[:, hi]), dot(bt[hi, :], bl[:, hi]))
    swap(1).start()
    for k in range(3):
        send_d(k).start()
    send_on(0)
    off = dot(bt[lo, :], bh[:, hi]) + (dot(bt[lo, :], bl[:, hi]) + dot(bt[hi, :], bl[:, lo]).T)
    for k in range(4, 8):
        i, j = BLOCKS[k]
        keep(k, off[i * T : i * T + T, (j - 2) * T : (j - 1) * T])
    swap(2).start()
    swap(3).start()
    for g in range(1, 4):
        send_on(g)

    def summed(g):
        if g == 0:
            for k in range(2):
                straight(k).wait_recv()
            fin[mine, 0] = (part[mine, 0] + recv_a[0]) + (recv_0[0] + recv_0[1])
        cross(g).wait_recv()
        group = crossing(g)
        fin[mine, group] = part[mine, group] + recv_b[group]
        share(g, mine).start()

    cycle = 2 * pair_count - 1
    now = round_ref[0]

    def wrap(value):
        return lax.rem(lax.rem(value, cycle) + cycle, cycle)

    top_id = jnp.where(pos == 0, 0, 1 + wrap(pos - 1 - now))
    bottom_id = 1 + wrap(2 * pair_count - 2 - pos - now)
    sign = jnp.where(top_id < bottom_id, 1.0, -1.0).astype(F32)
    along, down = [None] * 4, [None] * 4

    def diag_from(i, row):
        spread = jnp.where(on_diag, row, 0.0)
        along[i] = jnp.sum(spread, axis=0, keepdims=True)
        down[i] = jnp.sum(spread, axis=1, keepdims=True)

    def place(r, c, value):
        h, l = split(value)
        xh[r, c] = h
        xl[r, c] = l

    total = jnp.zeros((T, T), F32)
    summed(0)
    for k in range(3):
        send_d(k).wait_recv()
    d_last = (dv[0] + dv[1]) + (dv[2] + dv[3])
    for g in range(len(GROUPS)):
        if g + 1 < len(GROUPS):
            summed(g + 1)
        share(g, other).wait_recv()
        first, count = GROUPS[g]
        for k in range(first, first + count):
            i, j = BLOCKS[k]
            value = jnp.concatenate([fin[0, k], fin[1, k]], axis=0)
            if i == j:
                diag_from(i, value)
                diag_from(i + 1, d_last[g : g + 1, :])
                for m, side in ((i, upper), (i + 1, lower)):
                    s = value / (down[m] + along[m] + EPS)
                    s = jnp.where(side, s, 0.0)
                    if m > i:
                        s = -s
                    total = total + 2.0 * (s * s)
                    at = pl.ds(m * T, T)
                    place(at, at, s - s.T)
            else:
                si, sj = pl.ds(i * T, T), pl.ds(j * T, T)
                s = value / (down[i] + along[j] + EPS)
                if i < 2 <= j:
                    s = s * sign
                total = total + 2.0 * (s * s)
                place(si, sj, s)
                place(sj, si, -s.T)
    norm = 1.0 + jnp.sum(total, keepdims=True)
    scale = 1.0 / jnp.sqrt(norm)
    scale_sq = 1.0 / norm

    def put(r, c, value):
        h, l = split(value)
        ph[r, c] = h
        pm[r, c] = l

    def eye(size):
        return lax.broadcasted_iota(jnp.int32, (size, size), 0) == lax.broadcasted_iota(
            jnp.int32, (size, size), 1
        )

    narrow_eye = eye(width)
    for step in range(STEPS):
        weight = -0.5 * scale_sq if step == 0 else -0.5
        on = 1.5 - 0.5 * scale_sq if step == 0 else 1.5
        cross_part = dot_nt(xh[lo, :], xh[hi, :]) + (
            dot_nt(xh[lo, :], xl[hi, :]) + dot_nt(xl[lo, :], xh[hi, :])
        )
        cross_part = weight * cross_part
        put(lo, hi, cross_part)
        put(hi, lo, cross_part.T)
        for r in (lo, hi):
            m = dot_nt(xh[r, :], xl[r, :])
            square = dot_nt(xh[r, :], xh[r, :]) + (m + m.T)
            put(r, r, jnp.where(narrow_eye, on, 0.0) + weight * square)
        if step == 0:
            upper_part = dot(xh[lo, :], ph[...]) + (
                dot(xl[lo, :], ph[...]) + dot(xh[lo, :], pm[...])
            )
            last = dot(xh[hi, :], ph[:, hi]) + (
                dot(xl[hi, :], ph[:, hi]) + dot(xh[hi, :], pm[:, hi])
            )
            lower_part = jnp.concatenate([-upper_part[:, width:].T, last], axis=1)
            new = jnp.concatenate([upper_part, lower_part], axis=0)
        else:
            new = None
            for c in (lo, hi):
                more = dot(xh[:, c], ph[c, :]) + (
                    dot(xl[:, c], ph[c, :]) + dot(xh[:, c], pm[c, :])
                )
                new = more if new is None else new + more
        if step == 0:
            new = scale * (new + (ph[...].astype(F32) + pm[...].astype(F32)))
        h, l = split(new)
        xh[...] = h
        xl[...] = l

    def to_right(i, source=out_r):
        rs = pl.ds(i * step_rows, step_rows)
        return pltpu.make_async_remote_copy(
            source.at[rs], top.at[rs], r_send.at[i], r_recv.at[i],
            device_id=right, device_id_type=MESH,
        )

    def to_left(i):
        rs = pl.ds(i * step_rows, step_rows)
        return pltpu.make_async_remote_copy(
            out_l.at[rs], bot.at[rs], l_send.at[i], l_recv.at[i],
            device_id=left, device_id_type=MESH,
        )

    def rotated(i, columns):
        rs = pl.ds(pl.multiple_of(i * step_rows, step_rows), step_rows)
        h, l = bh[rs, :], bl[rs, :]
        w_h, w_l = xh[:, columns], xl[:, columns]
        return rs, dot(h, w_h) + (dot(h, w_l) + dot(l, w_h))

    def rotate_top(i, carry):
        rs, r = rotated(i, lo)
        out_r[rs, :] = r

        @pl.when(jnp.logical_and(has_left, has_right))
        def _():
            to_right(i).start()

        @pl.when(jnp.logical_not(has_right))
        def _():
            pltpu.make_async_copy(out_r.at[rs], bot.at[rs], l_recv.at[i]).start()

        @pl.when(jnp.logical_not(has_left))
        def _():
            pltpu.make_async_copy(out_r.at[rs], top.at[rs], r_recv.at[i]).start()

        return carry

    lax.fori_loop(0, CHUNKS, rotate_top, 0)

    def rotate_bottom(i, carry):
        rs, r = rotated(i, hi)
        out_l[rs, :] = r

        @pl.when(has_left)
        def _():
            to_left(i).start()

        @pl.when(jnp.logical_not(has_left))
        def _():
            to_right(i, out_l).start()

        return carry

    lax.fori_loop(0, CHUNKS, rotate_bottom, 0)

    for g in range(len(GROUPS)):
        swap(g).wait_send()
        cross(g).wait_send()
        share(g, mine).wait_send()
    for k in range(2):
        straight(k).wait_send()
    for k in range(3):
        send_d(k).wait_send()

    def finish(i, carry):
        @pl.when(has_right)
        def _():
            to_right(i).wait_send()

        @pl.when(has_left)
        def _():
            to_left(i).wait_send()

        to_right(i).wait_recv()
        to_left(i).wait_recv()
        return carry

    lax.fori_loop(0, CHUNKS, finish, 0)


def join(top, bot, out, sem):
    rows, width = top.shape
    copies = []
    for k in range(PIECES):
        rs = pl.ds(k * rows // PIECES, rows // PIECES)
        for i, half in enumerate((top, bot)):
            copies.append(
                pltpu.make_async_copy(
                    half.at[rs], out.at[rs, pl.ds(i * width, width)], sem.at[i, k]
                )
            )
    for copy in copies:
        copy.start()
    for copy in copies:
        copy.wait()


def shards(history, round_index):
    rows, cols = history.shape
    width = cols // 2
    vmem = pltpu.VMEM
    dma = pltpu.SemaphoreType.DMA
    top, bot = pl.pallas_call(
        kernel,
        out_shape=[jax.ShapeDtypeStruct((rows, width), F32)] * 2,
        in_specs=[
            pl.BlockSpec(memory_space=pltpu.SMEM),
            pl.BlockSpec(memory_space=pl.ANY),
        ],
        out_specs=[pl.BlockSpec(memory_space=pl.ANY)] * 2,
        scratch_shapes=[
            vmem((rows, cols), F32),
            vmem((rows, cols), BF16),
            vmem((rows, cols), BF16),
            vmem((cols, rows), BF16),
            vmem((2, len(BLOCKS), T // 2, T), F32),
            vmem((2, len(BLOCKS), T // 2, T), F32),
            vmem((len(BLOCKS), T // 2, T), F32),
            vmem((len(BLOCKS), T // 2, T), F32),
            vmem((2, T // 2, T), F32),
            vmem((4, 8, T), F32),
            vmem((cols, cols), BF16),
            vmem((cols, cols), BF16),
            vmem((cols, cols), BF16),
            vmem((cols, cols), BF16),
            vmem((rows, width), F32),
            vmem((rows, width), F32),
            dma((LOADS,)),
            dma((2, len(GROUPS))),
            dma((2, len(GROUPS))),
            dma((2, 2)),
            dma((2, len(GROUPS))),
            dma((2, 3)),
            dma((CHUNKS,)),
            dma((CHUNKS,)),
            dma((CHUNKS,)),
            dma((CHUNKS,)),
        ],
        compiler_params=pltpu.CompilerParams(
            collective_id=0, has_side_effects=True, vmem_limit_bytes=48 * 1024 * 1024
        ),
        name="pairing_round",
    )(round_index, history)
    return pl.pallas_call(
        join,
        out_shape=jax.ShapeDtypeStruct((rows, cols), F32),
        in_specs=[pl.BlockSpec(memory_space=pltpu.VMEM)] * 2,
        out_specs=pl.BlockSpec(memory_space=pl.ANY),
        scratch_shapes=[dma((2, PIECES))],
        compiler_params=pltpu.CompilerParams(vmem_limit_bytes=8 * 1024 * 1024),
        name="join",
    )(top, bot)


def solution(mesh):
    in_specs = (P("tm", "pair"), P())
    out_specs = P("tm", "pair")
    return jax.shard_map(shards, mesh=mesh, in_specs=in_specs, out_specs=out_specs, check_vma=False)
```
